32 devices in a mesh: groups: 2 (over y), gx: 4 (over z), gy: 2 (over x), gz: 2 (over core).
Axes of the slice: x: 2, y: 2, z: 4, core: 2. Of those that a mesh axis runs over, the one named last changes fastest.
Arguments:
- coords: float32 [8, 8, 16, 3, 128], P(('groups', 'gx'), 'gy', 'gz'), parts along dimension 0, may hold values from 0 to 1.1
- charges: float32 [8, 8, 16, 128], P(('groups', 'gx'), 'gy', 'gz'), parts along dimension 0, may hold values from -2 to 2
- atom_types: int32 [8, 8, 16, 128], P(('groups', 'gx'), 'gy', 'gz'), parts along dimension 0, may hold values from 0 to 63
- counts: int32 [8, 8, 16], P(('groups', 'gx'), 'gy', 'gz'), parts along dimension 0, may hold values from 64 to 128
- c6_table: float32 [64, 64], replicated, may hold values from 0.0001 to 0.001
- c12_table: float32 [64, 64], replicated, may hold values from 1e-08 to 1e-07
Outputs:
- forces: float32 [8, 8, 16, 3, 128], P(('groups', 'gx'), 'gy', 'gz'), parts along dimension 0
- energy: float32 [2], P('groups'), parts along dimension 0
The draws below stay inside these ranges and needn't reach their ends.
There are 2 independent parts, one for each index of `groups`. The reference program is written for one: setup_inputs(seed, part) draws one part's arguments, and reference() takes and returns one part's arrays. A program takes and returns all parts, laid end to end along the dimension named above; an argument that names none is the same for every part. Nothing has to cross between parts.
All inputs are finite; a program needn't handle non-finite values.
Results may differ from the reference program's by a relative error of at most 0.0003.
Values sent between devices are 32-bit elements; how exact they have to be, the bound alone decides.
A program may use at most 64 MiB of HBM per device.

```python
import math
import jax
import jax.numpy as jnp
from jax import lax

SLOTS = 128
TYPES = 64
NX = 4
NY = 8
NZ = 16


def set_ends(result, stream_key, low, top_value):
    index_at = [jax.random.randint(jax.random.fold_in(stream_key, axis), (), 0, length) for axis, length in enumerate(result.shape)]
    widest = result.shape.index(max(result.shape))
    beside = index_at[:widest] + [(index_at[widest] + 1) % result.shape[widest]] + index_at[widest + 1:]
    return result.at[tuple(index_at)].set(low).at[tuple(beside)].set(top_value)


def steps_of(key, extent, cuts, least, top_value):
    factor_of = 1.0
    for position, blocks in cuts:
        draws = jax.random.uniform(jax.random.fold_in(jax.random.fold_in(key, 6), position), (blocks,), jnp.float32, least / len(cuts), top_value / len(cuts))
        factor_of = factor_of * jnp.repeat(jnp.exp(draws), extent[position] // blocks).reshape((-1,) + (1,) * (len(extent) - 1 - position))
    return factor_of


def bell_draw(own_key, dims, scale, reach, split=(), kind=jnp.bfloat16):
    level = steps_of(own_key, dims, split, -0.22, 0.18) if split else 1.0
    result = jax.random.normal(own_key, dims, jnp.float32) * scale * level
    return jnp.minimum(jnp.maximum(result, -reach), reach).astype(kind)


def setup_inputs(seed: int = 0, part: int = 0) -> dict:
    streams_of = jax.random.split(jax.random.key(seed), 7)
    own_keys = jax.random.split(jax.random.fold_in(streams_of[6], part), 7)
    return {
        "coords": jnp.clip(1.1 * jax.random.uniform(own_keys[0], (NX, NY, NZ, 3, SLOTS), jnp.float32) ** steps_of(own_keys[0], (NX, NY, NZ, 3, SLOTS), ((0, 4), (1, 2), (2, 2)), -0.2, 0.2), 0.0, 1.1),
        "charges": bell_draw(own_keys[1], (NX, NY, NZ, SLOTS), 0.4, 2.0, ((0, 4), (1, 2), (2, 2)), jnp.float32),
        "atom_types": set_ends(jax.random.randint(own_keys[2], (NX, NY, NZ, SLOTS), 0, TYPES), jax.random.fold_in(own_keys[2], 1), 0, TYPES - 1).astype(jnp.int32),
        "counts": set_ends(jax.random.randint(own_keys[3], (NX, NY, NZ), SLOTS // 2, SLOTS + 1), jax.random.fold_in(own_keys[3], 1), SLOTS // 2, SLOTS).astype(jnp.int32),
        "c6_table": jnp.clip(jnp.exp(jax.random.uniform(streams_of[4], (TYPES, TYPES), jnp.float32, math.log(0.0001), math.log(0.001))), 0.0001, 0.001),
        "c12_table": jnp.clip(jnp.exp(jax.random.uniform(streams_of[5], (TYPES, TYPES), jnp.float32, math.log(9.99999993922529e-09), math.log(1.0000000116860974e-07))), 9.99999993922529e-09, 1.0000000116860974e-07),
    }


CELL_EDGE = 1.1
CUT_SQUARE = 1.0
SOFTEN = 0.09
ENERGY_UNIT = 0.1
CELL_PAIRS = ((0, 1), (0, 2), (0, 3), (0, 4), (0, 5), (0, 6), (0, 7), (1, 2), (1, 4), (2, 4), (1, 6), (2, 5), (4, 3))

def corner_bits(corner_index):
    return (corner_index >> 2 & 1, corner_index >> 1 & 1, corner_index & 1)

def pack_cells(coords, charges, atom_types, counts):
    slot_count = coords.shape[-1]
    occupied = (jnp.arange(slot_count, dtype=jnp.int32) < counts[..., None]).astype(jnp.float32)
    return jnp.concatenate([coords, charges[..., None, :], atom_types.astype(jnp.float32)[..., None, :], occupied[..., None, :]], axis=3)

def tile_terms(pack_a, pack_b, c6_sym, c12_sym, offset, pair_mask):
    type_ids = jnp.arange(c6_sym.shape[0]).astype(jnp.float32)
    type_hot_a = (pack_a[4][:, None] == type_ids[None, :]).astype(jnp.float32)
    type_hot_b = (pack_b[4][:, None] == type_ids[None, :]).astype(jnp.float32)
    c6_pair = jnp.dot(jnp.dot(type_hot_a, c6_sym, precision=lax.Precision.HIGHEST), type_hot_b.T, precision=lax.Precision.HIGHEST)
    c12_pair = jnp.dot(jnp.dot(type_hot_a, c12_sym, precision=lax.Precision.HIGHEST), type_hot_b.T, precision=lax.Precision.HIGHEST)
    charge_pair = pack_a[3][:, None] * pack_b[3][None, :]
    occupied_pair = pack_a[5][:, None] * pack_b[5][None, :] * pair_mask
    edge_inverse = 1.0 / (CUT_SQUARE + SOFTEN)
    edge_cube = edge_inverse ** 3

    def pair_energy(position_a, position_b):
        separation = position_b[:, None, :] - position_a[:, :, None] + offset[:, None, None]
        dist_square = lax.optimization_barrier(jnp.sum(separation * separation, axis=0))
        inverse = 1.0 / (dist_square + SOFTEN)
        inverse_cube = inverse * inverse * inverse
        coulomb = charge_pair * (jnp.sqrt(inverse) - edge_inverse ** 0.5)
        dispersion = c12_pair * (inverse_cube * inverse_cube - edge_cube * edge_cube) - c6_pair * (inverse_cube - edge_cube)
        cutoff_taper = jnp.maximum(1.0 - dist_square / CUT_SQUARE, 0.0)
        return ENERGY_UNIT * jnp.sum((coulomb + dispersion) * cutoff_taper * cutoff_taper * occupied_pair)
    energy, (grad_a, grad_b) = jax.value_and_grad(pair_energy, argnums=(0, 1))(pack_a[:3], pack_b[:3])
    return (energy, -grad_a, -grad_b)

def cell_batch(packs_a, packs_b, c6_sym, c12_sym, offset, pair_mask):

    def single(tiles):
        return tile_terms(tiles[0], tiles[1], c6_sym, c12_sym, offset, pair_mask)
    return lax.map(single, (packs_a, packs_b), batch_size=8)

def reference(coords, charges, atom_types, counts, c6_table, c12_table):
    c6_sym = 0.5 * (c6_table + c6_table.T)
    c12_sym = 0.5 * (c12_table + c12_table.T)
    packed = pack_cells(coords, charges, atom_types, counts)
    grid_shape = packed.shape[:3]
    slot_count = packed.shape[-1]
    upper_pairs = jnp.triu(jnp.ones((slot_count, slot_count), jnp.float32), 1)
    all_pairs = jnp.ones((slot_count, slot_count), jnp.float32)
    forces = jnp.zeros(grid_shape + (3, slot_count), jnp.float32)
    energy_sum = jnp.zeros((), jnp.float32)
    for source, target in ((0, 0),) + CELL_PAIRS:
        corner_a = corner_bits(source)
        corner_b = corner_bits(target)
        cells_a = jnp.roll(packed, (-corner_a[0], -corner_a[1], -corner_a[2]), axis=(0, 1, 2))
        cells_b = jnp.roll(packed, (-corner_b[0], -corner_b[1], -corner_b[2]), axis=(0, 1, 2))
        offset = jnp.array([(corner_b[k] - corner_a[k]) * CELL_EDGE for k in range(3)], jnp.float32)
        pair_mask = upper_pairs if source == target else all_pairs
        energies, force_a, force_b = cell_batch(cells_a.reshape((-1, 6, slot_count)), cells_b.reshape((-1, 6, slot_count)), c6_sym, c12_sym, offset, pair_mask)
        force_a = jnp.roll(force_a.reshape(grid_shape + (3, slot_count)), corner_a, axis=(0, 1, 2))
        force_b = jnp.roll(force_b.reshape(grid_shape + (3, slot_count)), corner_b, axis=(0, 1, 2))
        forces = forces + force_a + force_b
        energy_sum = energy_sum + jnp.sum(energies)
    return (forces, energy_sum.reshape(1))
```

```python
import functools

import jax
import jax.numpy as jnp
from jax import lax
from jax.experimental import pallas as pl
from jax.experimental.pallas import tpu as pltpu
from jax.sharding import PartitionSpec as P

CELL_EDGE = 1.1
SOFTEN = 0.09
ENERGY_UNIT = 0.1
EDGE_V = 1.0 / (1.0 + SOFTEN)
E0 = EDGE_V**0.5
E3 = EDGE_V**3
UNROLL = 4
GROUPS = (
    ((1, -1, -1, 3), (1, 0, -1, 3), (0, 0, 0, 2)),
    ((1, 1, -1, 3), (0, 1, -1, 3)),
)
SELF_ROW = 6


def shifted(block, axis, distance):
    n = lax.axis_size(axis)
    route = [((i - distance) % n, i) for i in range(n)]
    return lax.ppermute(block, axis, route)


def from_both(first, last, axis):
    if lax.axis_size(axis) == 2:
        both = shifted(jnp.stack([first, last]), axis, 1)
        return both[0], both[1]
    return shifted(first, axis, -1), shifted(last, axis, 1)


def pair_kernel(cx, cy, cz, nt, scal_ref, type_ref, count_ref, ext_ref, c6_ref, c12_ref,
                force_ref, energy_ref, tcell, table, fa):
    ey = cy + 2
    ez = cz + 2
    slots = 128
    force_ref[...] = jnp.zeros_like(force_ref)
    fa[...] = jnp.zeros_like(fa)
    table[...] = jnp.zeros_like(table)
    c6 = c6_ref[...]
    c12 = c12_ref[...]
    c6 = (0.5 * ENERGY_UNIT) * (c6 + c6.T)
    c12 = (0.5 * ENERGY_UNIT) * (c12 + c12.T)
    both = jnp.concatenate([c12, c6], axis=0)
    high = both.astype(jnp.bfloat16)
    low = (both - high.astype(jnp.float32)).astype(jnp.bfloat16)
    left = jnp.concatenate([high, low], axis=1)
    ids = lax.broadcasted_iota(jnp.int32, (nt, slots), 0).astype(jnp.float32)

    def table_of(xy, carry):
        for z in range(ez):
            row = ext_ref[4, xy, z : z + 1, :]
            hot = (ids == row).astype(jnp.float32).astype(jnp.bfloat16)
            tcell[xy, z] = jnp.dot(
                left, jnp.concatenate([hot, hot], axis=0), preferred_element_type=jnp.float32
            )
        return carry

    lax.fori_loop(1, (cx + 1) * ey, table_of, 0)

    rows = lax.broadcasted_iota(jnp.int32, (8, slots), 0)
    lanes = lax.broadcasted_iota(jnp.int32, (8, slots), 1)
    self_lane = jnp.where(rows == SELF_ROW, lanes, slots)
    ones = jnp.ones((8, slots), jnp.float32)

    def cell(c, e_sum):
        x = c // (cy * cz)
        y = (c // cz) % cy
        z = c % cz
        b_rows = []
        for g, runs in enumerate(GROUPS):
            comps = [[], [], [], []]
            r = 0
            for ox, oy, oz, length in runs:
                xy = (x + ox) * ey + y + 1 + oy
                z0 = z + 1 + oz
                for k in range(4):
                    comps[k].append(ext_ref[k, xy, pl.ds(z0, length), :])
                for j in range(length):
                    t = tcell.at[xy, z0 + j]
                    table[pl.ds(8 * g + r, nt, stride=32), :] = t[:nt, :]
                    table[pl.ds(16 + 8 * g + r, nt, stride=32), :] = t[nt:, :]
                    r += 1
            if r < 8:
                for k in range(4):
                    comps[k].append(jnp.zeros((8 - r, slots), jnp.float32))
            full = [jnp.concatenate(p, axis=0) for p in comps]
            for k in range(3):
                off = jnp.zeros((8, slots), jnp.float32)
                r = 0
                for ox, oy, oz, length in runs:
                    for j in range(length):
                        o = (ox, oy, oz + j)[k]
                        if o:
                            off = jnp.where(rows == r, jnp.float32(o * CELL_EDGE), off)
                        r += 1
                full[k] = full[k] + off
            full[3] = full[3] * ENERGY_UNIT
            b_rows.append(full)
        n_atoms = count_ref[c]

        def atoms(step, carry):
            acc = [list(carry[0:3]), list(carry[3:6])]
            e_acc = carry[6]
            for uu in range(UNROLL):
                i = step * UNROLL + uu
                at = c * (4 * slots) + i
                xi = scal_ref[at]
                yi = scal_ref[at + slots]
                zi = scal_ref[at + 2 * slots]
                qi = scal_ref[at + 3 * slots]
                ti = pl.multiple_of(type_ref[c * slots + i] * 32, 32)
                mine = None
                for g in range(2):
                    bx, by, bz, bq = b_rows[g]
                    c12p = table[pl.ds(ti + 8 * g, 8), :]
                    c6p = table[pl.ds(ti + 16 + 8 * g, 8), :]
                    dx = bx - xi
                    dy = by - yi
                    dz = bz - zi
                    t = dx * dx + dy * dy + (dz * dz + SOFTEN)
                    s = lax.rsqrt(t)
                    v = s * s
                    z3 = v * v * v
                    w = jnp.maximum((1.0 + SOFTEN) - t, 0.0)
                    if g == 0:
                        w = jnp.where(self_lane > i, w, 0.0)
                    qq = bq * qi
                    cz12 = c12p * z3
                    y1 = cz12 - c6p
                    u = qq * (s - E0) + (z3 - E3) * (y1 + c12p * E3)
                    h = qq * s + (z3 * 6.0) * (y1 + cz12)
                    uw = u * w
                    e_acc = e_acc + uw * w
                    gg = w * (v * h * w) + 4.0 * uw
                    f = [gg * dx, gg * dy, gg * dz]
                    acc[g] = [p + q for p, q in zip(acc[g], f)]
                    mine = f if mine is None else [p + q for p, q in zip(mine, f)]
                for k in range(3):
                    fa[k, pl.ds(pl.multiple_of(i * 8, 8), 8), :] = mine[k]
            return (*acc[0], *acc[1], e_acc)

        zero = jnp.zeros((8, slots), jnp.float32)
        out = lax.fori_loop(0, (n_atoms + UNROLL - 1) // UNROLL, atoms, (zero,) * 6 + (e_sum,))
        for g, runs in enumerate(GROUPS):
            r = 0
            for ox, oy, oz, length in runs:
                xy = (x + ox) * ey + y + 1 + oy
                for k in range(3):
                    force_ref[k, xy, pl.ds(z + 1 + oz, length), :] += out[3 * g + k][r : r + length]
                r += length
        occupied = lax.broadcasted_iota(jnp.int32, (1, slots), 1) < n_atoms
        for k in range(3):
            total = fa[k, pl.ds(0, slots, stride=8), :]
            for s in range(1, 8):
                total = total + fa[k, pl.ds(s, slots, stride=8), :]
            summed = lax.dot_general(
                ones, total, (((1,), (1,)), ((), ())),
                precision=lax.Precision.HIGHEST, preferred_element_type=jnp.float32,
            )[:1]
            force_ref[k, x * ey + y + 1, pl.ds(z + 1, 1), :] -= jnp.where(occupied, summed, 0.0)
        return out[6]

    e = lax.fori_loop(0, cx * cy * cz, cell, jnp.zeros((8, slots), jnp.float32))
    energy_ref[...] = e


def on_device(coords, charges, atom_types, counts, c6_table, c12_table):
    cx, cy, cz, _, slots = coords.shape
    nt = c6_table.shape[0]
    occ = jnp.arange(slots, dtype=jnp.int32) < counts[..., None]
    charge = jnp.where(occ, charges, 0.0)
    kind = jnp.where(occ, atom_types, nt)
    local = jnp.concatenate(
        [jnp.moveaxis(coords, 3, 0), charge[None], kind.astype(jnp.float32)[None]], axis=0
    )
    scal = jnp.concatenate([coords, charge[..., None, :]], axis=3).reshape(-1)
    up = shifted(local[:, :1], "gx", -1)
    ext = jnp.concatenate([local, up], axis=1)
    above, below = from_both(ext[:, :, :1], ext[:, :, -1:], "gy")
    ext = jnp.concatenate([below, ext, above], axis=2)
    above, below = from_both(ext[:, :, :, :1], ext[:, :, :, -1:], "gz")
    ext = jnp.concatenate([below, ext, above], axis=3)
    ex, ey, ez = cx + 1, cy + 2, cz + 2
    vm = pl.BlockSpec(memory_space=pltpu.VMEM)
    sm = pl.BlockSpec(memory_space=pltpu.SMEM)
    forces, energy = pl.pallas_call(
        functools.partial(pair_kernel, cx, cy, cz, nt),
        out_shape=(
            jax.ShapeDtypeStruct((3, ex * ey, ez, slots), jnp.float32),
            jax.ShapeDtypeStruct((8, slots), jnp.float32),
        ),
        in_specs=[sm, sm, sm, vm, vm, vm],
        out_specs=(vm, vm),
        scratch_shapes=[
            pltpu.VMEM((ex * ey, ez, 2 * nt, slots), jnp.float32),
            pltpu.VMEM(((nt + 1) * 32, slots), jnp.float32),
            pltpu.VMEM((3, slots * 8, slots), jnp.float32),
        ],
        compiler_params=pltpu.CompilerParams(vmem_limit_bytes=48 * 2**20),
    )(scal, kind.reshape(-1), counts.reshape(-1), ext.reshape(5, ex * ey, ez, slots), c6_table, c12_table)
    energies = lax.all_gather(jnp.sum(energy).reshape(1), ("gx", "gy", "gz"), tiled=True)
    forces = forces.reshape(3, ex, ey, ez, slots)
    low, high = from_both(forces[:, :, :, :1], forces[:, :, :, -1:], "gz")
    forces = forces[:, :, :, 1:-1].at[:, :, :, -1:].add(low).at[:, :, :, :1].add(high)
    low, high = from_both(forces[:, :, :1], forces[:, :, -1:], "gy")
    forces = forces[:, :, 1:-1].at[:, :, -1:].add(low).at[:, :, :1].add(high)
    back = shifted(forces[:, cx:], "gx", 1)
    forces = forces[:, :cx].at[:, :1].add(back)
    return jnp.moveaxis(forces, 0, 3), jnp.sum(energies).reshape(1)


def solution(mesh):
    return jax.shard_map(
        on_device,
        mesh=mesh,
        in_specs=(
            P(("groups", "gx"), "gy", "gz", None, None),
            P(("groups", "gx"), "gy", "gz", None),
            P(("groups", "gx"), "gy", "gz", None),
            P(("groups", "gx"), "gy", "gz"),
            P(),
            P(),
        ),
        out_specs=(P(("groups", "gx"), "gy", "gz", None, None), P("groups")),
        check_vma=False,
    )
```

```python
import functools

import jax
import jax.numpy as jnp
from jax import lax
from jax.experimental import pallas as pl
from jax.experimental.pallas import tpu as pltpu
from jax.sharding import PartitionSpec as P

CELL_EDGE = 1.1
SOFTEN = 0.09
ENERGY_UNIT = 0.1
EDGE_V = 1.0 / (1.0 + SOFTEN)
E0 = EDGE_V**0.5
E3 = EDGE_V**3
UNROLL = 8
GROUPS = (
    ((1, -1, -1, 3), (1, 0, -1, 3), (0, 0, 0, 2)),
    ((1, 1, -1, 3), (0, 1, -1, 3)),
)
SELF_ROW = 6


def shifted(block, axis, distance):
    n = lax.axis_size(axis)
    route = [((i - distance) % n, i) for i in range(n)]
    return lax.ppermute(block, axis, route)


def from_both(first, last, axis):
    if lax.axis_size(axis) == 2:
        both = shifted(jnp.stack([first, last]), axis, 1)
        return both[0], both[1]
    return shifted(first, axis, -1), shifted(last, axis, 1)


def ring_sum(value, axis):
    total = value
    for distance in range(1, lax.axis_size(axis)):
        total = total + shifted(value, axis, distance)
    return total


def returned(first, last, energy, axis):
    if lax.axis_size(axis) != 2:
        return (*from_both(first, last, axis), ring_sum(energy, axis))
    slots = energy.shape[-1]
    rows = jnp.stack([first, last]).reshape(-1, slots)
    got = shifted(jnp.concatenate([rows, energy]), axis, 1)
    both = got[:-1].reshape(2, *first.shape)
    return both[0], both[1], energy + got[-1:]


def pair_kernel(cx, cy, cz, nt, scal_ref, type_ref, count_ref, ext_ref, c6_ref, c12_ref,
                force_ref, energy_ref, tcell, table, fa, columns, flat):
    ey = cy + 2
    ez = cz + 2
    slots = 128
    force_ref[...] = jnp.zeros_like(force_ref)
    fa[...] = jnp.zeros_like(fa)
    table[...] = jnp.zeros_like(table)
    c6 = c6_ref[...]
    c12 = c12_ref[...]
    c6 = (0.5 * ENERGY_UNIT) * (c6 + c6.T)
    c12 = (0.5 * ENERGY_UNIT) * (c12 + c12.T)
    both = jnp.concatenate([c12, c6], axis=0)
    high = both.astype(jnp.bfloat16)
    low = (both - high.astype(jnp.float32)).astype(jnp.bfloat16)
    left = jnp.concatenate([high, low], axis=1)
    ids = lax.broadcasted_iota(jnp.int32, (nt, slots), 0).astype(jnp.float32)

    def table_of(xy, carry):
        for z in range(ez):
            row = ext_ref[4, xy, z : z + 1, :]
            hot = (ids == row).astype(jnp.float32).astype(jnp.bfloat16)
            tcell[xy, z] = jnp.dot(
                left, jnp.concatenate([hot, hot], axis=0), preferred_element_type=jnp.float32
            )
        return carry

    lax.fori_loop(1, (cx + 1) * ey, table_of, 0)

    rows = lax.broadcasted_iota(jnp.int32, (8, slots), 0)
    lanes = lax.broadcasted_iota(jnp.int32, (8, slots), 1)
    self_lane = jnp.where(rows == SELF_ROW, lanes, slots)
    wide_lanes = lax.broadcasted_iota(jnp.int32, (slots, slots), 1)
    columns[...] = jnp.zeros_like(columns)

    def cell(c, e_sum):
        x = c // (cy * cz)
        y = (c // cz) % cy
        z = c % cz
        b_rows = []
        for g, runs in enumerate(GROUPS):
            comps = [[], [], [], []]
            r = 0
            for ox, oy, oz, length in runs:
                xy = (x + ox) * ey + y + 1 + oy
                z0 = z + 1 + oz
                for k in range(4):
                    comps[k].append(ext_ref[k, xy, pl.ds(z0, length), :])
                for j in range(length):
                    t = tcell.at[xy, z0 + j]
                    table[pl.ds(8 * g + r, nt, stride=32), :] = t[:nt, :]
                    table[pl.ds(16 + 8 * g + r, nt, stride=32), :] = t[nt:, :]
                    r += 1
            if r < 8:
                for k in range(4):
                    comps[k].append(jnp.zeros((8 - r, slots), jnp.float32))
            full = [jnp.concatenate(p, axis=0) for p in comps]
            for k in range(3):
                off = jnp.zeros((8, slots), jnp.float32)
                r = 0
                for ox, oy, oz, length in runs:
                    for j in range(length):
                        o = (ox, oy, oz + j)[k]
                        if o:
                            off = jnp.where(rows == r, jnp.float32(o * CELL_EDGE), off)
                        r += 1
                full[k] = full[k] + off
            full[3] = full[3] * ENERGY_UNIT
            b_rows.append(full)
        n_atoms = count_ref[c]

        def atoms(step, carry):
            acc = [list(carry[0:3]), list(carry[3:6])]
            e_acc = carry[6]
            for uu in range(UNROLL):
                i = step * UNROLL + uu
                at = c * (4 * slots) + i
                xi = scal_ref[at]
                yi = scal_ref[at + slots]
                zi = scal_ref[at + 2 * slots]
                qi = scal_ref[at + 3 * slots]
                ti = pl.multiple_of(type_ref[c * slots + i] * 32, 32)
                mine = None
                for g in range(2):
                    bx, by, bz, bq = b_rows[g]
                    c12p = table[pl.ds(ti + 8 * g, 8), :]
                    c6p = table[pl.ds(ti + 16 + 8 * g, 8), :]
                    dx = bx - xi
                    dy = by - yi
                    dz = bz - zi
                    t = dx * dx + dy * dy + (dz * dz + SOFTEN)
                    s = lax.rsqrt(t)
                    v = s * s
                    z3 = v * v * v
                    w = jnp.maximum((1.0 + SOFTEN) - t, 0.0)
                    if g == 0:
                        w = jnp.where(self_lane > i, w, 0.0)
                    qq = bq * qi
                    cz12 = c12p * z3
                    y1 = cz12 - c6p
                    u = qq * (s - E0) + (z3 - E3) * (y1 + c12p * E3)
                    h = qq * s + (z3 * 6.0) * (y1 + cz12)
                    uw = u * w
                    e_acc = e_acc + uw * w
                    gg = w * (v * h * w) + 4.0 * uw
                    f = [gg * dx, gg * dy, gg * dz]
                    acc[g] = [p + q for p, q in zip(acc[g], f)]
                    mine = f if mine is None else [p + q for p, q in zip(mine, f)]
                for k in range(3):
                    fa[k, pl.ds(pl.multiple_of(i * 8, 8), 8), :] = mine[k]
            return (*acc[0], *acc[1], e_acc)

        zero = jnp.zeros((8, slots), jnp.float32)
        out = lax.fori_loop(0, (n_atoms + UNROLL - 1) // UNROLL, atoms, (zero,) * 6 + (e_sum,))
        for g, runs in enumerate(GROUPS):
            r = 0
            for ox, oy, oz, length in runs:
                xy = (x + ox) * ey + y + 1 + oy
                for k in range(3):
                    force_ref[k, xy, pl.ds(z + 1 + oz, length), :] += out[3 * g + k][r : r + length]
                r += length
        mine_lane = wide_lanes == c % slots
        for k in range(3):
            total = fa[k, pl.ds(0, slots, stride=8), :]
            for s in range(1, 8):
                total = total + fa[k, pl.ds(s, slots, stride=8), :]
            summed = jnp.sum(total, axis=1, keepdims=True)
            columns[k, c // slots] = jnp.where(mine_lane, summed, columns[k, c // slots])
        return out[6]

    n_cells = cx * cy * cz
    e = lax.fori_loop(0, n_cells, cell, jnp.zeros((8, slots), jnp.float32))
    energy_ref[...] = e
    for k in range(3):
        for part in range(columns.shape[1]):
            flat[pl.ds(part * slots, slots), :] = columns[k, part].T
        for xy in range(cx * cy):
            at = (xy // cy) * ey + xy % cy + 1
            for z in range(cz):
                c = xy * cz + z
                occupied = lanes[:1] < count_ref[c]
                force_ref[k, at, z + 1 : z + 2, :] -= jnp.where(occupied, flat[c : c + 1, :], 0.0)


def on_device(coords, charges, atom_types, counts, c6_table, c12_table):
    cx, cy, cz, _, slots = coords.shape
    nt = c6_table.shape[0]
    occ = jnp.arange(slots, dtype=jnp.int32) < counts[..., None]
    charge = jnp.where(occ, charges, 0.0)
    kind = jnp.where(occ, atom_types, nt)
    local = jnp.concatenate(
        [jnp.moveaxis(coords, 3, 0), charge[None], kind.astype(jnp.float32)[None]], axis=0
    )
    scal = jnp.concatenate([coords, charge[..., None, :]], axis=3).reshape(-1)
    up = shifted(local[:, :1], "gx", -1)
    ext = jnp.concatenate([local, up], axis=1)
    above, below = from_both(ext[:, :, :1], ext[:, :, -1:], "gy")
    ext = jnp.concatenate([below, ext, above], axis=2)
    above, below = from_both(ext[:, :, :, :1], ext[:, :, :, -1:], "gz")
    ext = jnp.concatenate([below, ext, above], axis=3)
    parts = (cx * cy * cz + slots - 1) // slots
    ex, ey, ez = cx + 1, cy + 2, cz + 2
    vm = pl.BlockSpec(memory_space=pltpu.VMEM)
    sm = pl.BlockSpec(memory_space=pltpu.SMEM)
    forces, energy = pl.pallas_call(
        functools.partial(pair_kernel, cx, cy, cz, nt),
        out_shape=(
            jax.ShapeDtypeStruct((3, ex * ey, ez, slots), jnp.float32),
            jax.ShapeDtypeStruct((8, slots), jnp.float32),
        ),
        in_specs=[sm, sm, sm, vm, vm, vm],
        out_specs=(vm, vm),
        scratch_shapes=[
            pltpu.VMEM((ex * ey, ez, 2 * nt, slots), jnp.float32),
            pltpu.VMEM(((nt + 1) * 32, slots), jnp.float32),
            pltpu.VMEM((3, slots * 8, slots), jnp.float32),
            pltpu.VMEM((3, parts, slots, slots), jnp.float32),
            pltpu.VMEM((parts * slots, slots), jnp.float32),
        ],
        compiler_params=pltpu.CompilerParams(vmem_limit_bytes=48 * 2**20),
    )(scal, kind.reshape(-1), counts.reshape(-1), ext.reshape(5, ex * ey, ez, slots), c6_table, c12_table)
    energy = jnp.sum(energy, axis=0, keepdims=True)
    forces = forces.reshape(3, ex, ey, ez, slots)
    low, high, energy = returned(forces[:, :, :, :1], forces[:, :, :, -1:], energy, "gz")
    forces = forces[:, :, :, 1:-1].at[:, :, :, -1:].add(low).at[:, :, :, :1].add(high)
    low, high, energy = returned(forces[:, :, :1], forces[:, :, -1:], energy, "gy")
    forces = forces[:, :, 1:-1].at[:, :, -1:].add(low).at[:, :, :1].add(high)
    back = shifted(forces[:, cx:], "gx", 1)
    forces = forces[:, :cx].at[:, :1].add(back)
    energy = jnp.sum(ring_sum(energy, "gx"))
    return jnp.moveaxis(forces, 0, 3), energy.reshape(1)


def solution(mesh):
    return jax.shard_map(
        on_device,
        mesh=mesh,
        in_specs=(
            P(("groups", "gx"), "gy", "gz", None, None),
            P(("groups", "gx"), "gy", "gz", None),
            P(("groups", "gx"), "gy", "gz", None),
            P(("groups", "gx"), "gy", "gz"),
            P(),
            P(),
        ),
        out_specs=(P(("groups", "gx"), "gy", "gz", None, None), P("groups")),
        check_vma=False,
    )
```

```python
import functools

import jax
import jax.numpy as jnp
from jax import lax
from jax.experimental import pallas as pl
from jax.experimental.pallas import tpu as pltpu
from jax.sharding import PartitionSpec as P

CELL_EDGE = 1.1
SOFTEN = 0.09
ENERGY_UNIT = 0.1
EDGE_V = 1.0 / (1.0 + SOFTEN)
E0 = EDGE_V**0.5
E3 = EDGE_V**3
UNROLL = 8
GROUPS = (
    ((1, -1, -1, 3), (1, 0, -1, 3), (0, 0, 0, 2)),
    ((1, 1, -1, 3), (0, 1, -1, 3)),
)
SELF_ROW = 6


def shifted(block, axis, distance):
    n = lax.axis_size(axis)
    route = [((i - distance) % n, i) for i in range(n)]
    return lax.ppermute(block, axis, route)


def from_both(first, last, axis):
    if lax.axis_size(axis) == 2:
        both = shifted(jnp.stack([first, last]), axis, 1)
        return both[0], both[1]
    return shifted(first, axis, -1), shifted(last, axis, 1)


def ring_sum(value, axis):
    total = value
    for distance in range(1, lax.axis_size(axis)):
        total = total + shifted(value, axis, distance)
    return total


def returned(first, last, energy, axis):
    if lax.axis_size(axis) != 2:
        return (*from_both(first, last, axis), ring_sum(energy, axis))
    slots = energy.shape[-1]
    rows = jnp.stack([first, last]).reshape(-1, slots)
    got = shifted(jnp.concatenate([rows, energy]), axis, 1)
    both = got[:-1].reshape(2, *first.shape)
    return both[0], both[1], energy + got[-1:]


def pair_kernel(cx, cy, cz, nt, scal_ref, type_ref, count_ref, ext_ref, c6_ref, c12_ref,
                force_ref, energy_ref, tcell, table, fa, fb, columns, flat):
    ey = cy + 2
    ez = cz + 2
    slots = 128
    force_ref[...] = jnp.zeros_like(force_ref)
    fa[...] = jnp.zeros_like(fa)
    fb[...] = jnp.zeros_like(fb)
    table[...] = jnp.zeros_like(table)
    c6 = c6_ref[...]
    c12 = c12_ref[...]
    c6 = (0.5 * ENERGY_UNIT) * (c6 + c6.T)
    c12 = (0.5 * ENERGY_UNIT) * (c12 + c12.T)
    both = jnp.concatenate([c12, c6], axis=0)
    high = both.astype(jnp.bfloat16)
    low = (both - high.astype(jnp.float32)).astype(jnp.bfloat16)
    left = jnp.concatenate([high, low], axis=1)
    ids = lax.broadcasted_iota(jnp.int32, (nt, slots), 0).astype(jnp.float32)

    def table_of(xy, carry):
        for z in range(ez):
            row = ext_ref[4, xy, z : z + 1, :]
            hot = (ids == row).astype(jnp.float32).astype(jnp.bfloat16)
            tcell[xy, z] = jnp.dot(
                left, jnp.concatenate([hot, hot], axis=0), preferred_element_type=jnp.float32
            )
        return carry

    lax.fori_loop(1, (cx + 1) * ey, table_of, 0)

    rows = lax.broadcasted_iota(jnp.int32, (8, slots), 0)
    lanes = lax.broadcasted_iota(jnp.int32, (8, slots), 1)
    self_lane = jnp.where(rows == SELF_ROW, lanes, slots)
    wide_lanes = lax.broadcasted_iota(jnp.int32, (slots, slots), 1)
    columns[...] = jnp.zeros_like(columns)

    def cell(c, e_sum):
        x = c // (cy * cz)
        y = (c // cz) % cy
        z = c % cz
        b_rows = []
        for g, runs in enumerate(GROUPS):
            comps = [[], [], [], []]
            r = 0
            for ox, oy, oz, length in runs:
                xy = (x + ox) * ey + y + 1 + oy
                z0 = z + 1 + oz
                for k in range(4):
                    comps[k].append(ext_ref[k, xy, pl.ds(z0, length), :])
                for j in range(length):
                    t = tcell.at[xy, z0 + j]
                    table[g, pl.ds(r, nt, stride=8), :] = t[:nt, :]
                    table[2 + g, pl.ds(r, nt, stride=8), :] = t[nt:, :]
                    r += 1
            if r < 8:
                for k in range(4):
                    comps[k].append(jnp.zeros((8 - r, slots), jnp.float32))
            full = [jnp.concatenate(p, axis=0) for p in comps]
            for k in range(3):
                off = jnp.zeros((8, slots), jnp.float32)
                r = 0
                for ox, oy, oz, length in runs:
                    for j in range(length):
                        o = (ox, oy, oz + j)[k]
                        if o:
                            off = jnp.where(rows == r, jnp.float32(o * CELL_EDGE), off)
                        r += 1
                full[k] = full[k] + off
            full[3] = full[3] * ENERGY_UNIT
            b_rows.append(full)
        n_atoms = count_ref[c]

        def fold(step):
            at = pl.ds(pl.multiple_of(step * UNROLL, UNROLL), UNROLL)
            for k in range(3):
                total = fa[k, pl.ds(0, UNROLL, stride=8), :]
                for s in range(1, 8):
                    total = total + fa[k, pl.ds(s, UNROLL, stride=8), :]
                fb[k, at, :] = total

        def atoms(step, carry):
            fold(step)
            acc = [list(carry[0:3]), list(carry[3:6])]
            e_acc = carry[6]
            for uu in range(UNROLL):
                i = step * UNROLL + uu
                at = c * (4 * slots) + i
                xi = scal_ref[at]
                yi = scal_ref[at + slots]
                zi = scal_ref[at + 2 * slots]
                qi = scal_ref[at + 3 * slots]
                ti = pl.multiple_of(type_ref[c * slots + i] * 8, 8)
                mine = None
                for g in range(2):
                    bx, by, bz, bq = b_rows[g]
                    c12p = table[g, pl.ds(ti, 8), :]
                    c6p = table[2 + g, pl.ds(ti, 8), :]
                    dx = bx - xi
                    dy = by - yi
                    dz = bz - zi
                    t = dx * dx + dy * dy + (dz * dz + SOFTEN)
                    s = lax.rsqrt(t)
                    v = s * s
                    z3 = v * v * v
                    w = jnp.maximum((1.0 + SOFTEN) - t, 0.0)
                    if g == 0:
                        w = jnp.where(self_lane > i, w, 0.0)
                    qq = bq * qi
                    cz12 = c12p * z3
                    y1 = cz12 - c6p
                    u = qq * (s - E0) + (z3 - E3) * (y1 + c12p * E3)
                    h = qq * s + (z3 * 6.0) * (y1 + cz12)
                    uw = u * w
                    e_acc = e_acc + uw * w
                    gg = w * (v * h * w) + 4.0 * uw
                    f = [gg * dx, gg * dy, gg * dz]
                    acc[g] = [p + q for p, q in zip(acc[g], f)]
                    mine = f if mine is None else [p + q for p, q in zip(mine, f)]
                for k in range(3):
                    fa[k, pl.ds(uu * 8, 8), :] = mine[k]
            return (*acc[0], *acc[1], e_acc)

        zero = jnp.zeros((8, slots), jnp.float32)
        steps = (n_atoms + UNROLL - 1) // UNROLL
        out = lax.fori_loop(0, steps, atoms, (zero,) * 6 + (e_sum,))
        fold(steps)
        for g, runs in enumerate(GROUPS):
            r = 0
            for ox, oy, oz, length in runs:
                xy = (x + ox) * ey + y + 1 + oy
                for k in range(3):
                    force_ref[k, xy, pl.ds(z + 1 + oz, length), :] += out[3 * g + k][r : r + length]
                r += length
        mine_lane = wide_lanes == c % slots
        for k in range(3):
            summed = jnp.sum(fb[k, pl.ds(UNROLL, slots), :], axis=1, keepdims=True)
            columns[k, c // slots] = jnp.where(mine_lane, summed, columns[k, c // slots])
        return out[6]

    n_cells = cx * cy * cz
    e = lax.fori_loop(0, n_cells, cell, jnp.zeros((8, slots), jnp.float32))
    energy_ref[...] = e
    for k in range(3):
        for part in range(columns.shape[1]):
            flat[pl.ds(part * slots, slots), :] = columns[k, part].T
        for xy in range(cx * cy):
            at = (xy // cy) * ey + xy % cy + 1
            for z in range(cz):
                c = xy * cz + z
                occupied = lanes[:1] < count_ref[c]
                force_ref[k, at, z + 1 : z + 2, :] -= jnp.where(occupied, flat[c : c + 1, :], 0.0)


def on_device(coords, charges, atom_types, counts, c6_table, c12_table):
    cx, cy, cz, _, slots = coords.shape
    nt = c6_table.shape[0]
    occ = jnp.arange(slots, dtype=jnp.int32) < counts[..., None]
    charge = jnp.where(occ, charges, 0.0)
    kind = jnp.where(occ, atom_types, nt)
    local = jnp.concatenate(
        [jnp.moveaxis(coords, 3, 0), charge[None], kind.astype(jnp.float32)[None]], axis=0
    )
    scal = jnp.concatenate([coords, charge[..., None, :]], axis=3).reshape(-1)
    up = shifted(local[:, :1], "gx", -1)
    ext = jnp.concatenate([local, up], axis=1)
    above, below = from_both(ext[:, :, :1], ext[:, :, -1:], "gy")
    ext = jnp.concatenate([below, ext, above], axis=2)
    above, below = from_both(ext[:, :, :, :1], ext[:, :, :, -1:], "gz")
    ext = jnp.concatenate([below, ext, above], axis=3)
    parts = (cx * cy * cz + slots - 1) // slots
    ex, ey, ez = cx + 1, cy + 2, cz + 2
    vm = pl.BlockSpec(memory_space=pltpu.VMEM)
    sm = pl.BlockSpec(memory_space=pltpu.SMEM)
    forces, energy = pl.pallas_call(
        functools.partial(pair_kernel, cx, cy, cz, nt),
        out_shape=(
            jax.ShapeDtypeStruct((3, ex * ey, ez, slots), jnp.float32),
            jax.ShapeDtypeStruct((8, slots), jnp.float32),
        ),
        in_specs=[sm, sm, sm, vm, vm, vm],
        out_specs=(vm, vm),
        scratch_shapes=[
            pltpu.VMEM((ex * ey, ez, 2 * nt, slots), jnp.float32),
            pltpu.VMEM((4, (nt + 1) * 8, slots), jnp.float32),
            pltpu.VMEM((3, UNROLL * 8, slots), jnp.float32),
            pltpu.VMEM((3, UNROLL + slots, slots), jnp.float32),
            pltpu.VMEM((3, parts, slots, slots), jnp.float32),
            pltpu.VMEM((parts * slots, slots), jnp.float32),
        ],
        compiler_params=pltpu.CompilerParams(vmem_limit_bytes=48 * 2**20),
    )(scal, kind.reshape(-1), counts.reshape(-1), ext.reshape(5, ex * ey, ez, slots), c6_table, c12_table)
    energy = jnp.sum(energy, axis=0, keepdims=True)
    forces = forces.reshape(3, ex, ey, ez, slots)
    low, high, energy = returned(forces[:, :, :, :1], forces[:, :, :, -1:], energy, "gz")
    forces = forces[:, :, :, 1:-1].at[:, :, :, -1:].add(low).at[:, :, :, :1].add(high)
    low, high, energy = returned(forces[:, :, :1], forces[:, :, -1:], energy, "gy")
    forces = forces[:, :, 1:-1].at[:, :, -1:].add(low).at[:, :, :1].add(high)
    back = shifted(forces[:, cx:], "gx", 1)
    forces = forces[:, :cx].at[:, :1].add(back)
    energy = jnp.sum(ring_sum(energy, "gx"))
    return jnp.moveaxis(forces, 0, 3), energy.reshape(1)


def solution(mesh):
    return jax.shard_map(
        on_device,
        mesh=mesh,
        in_specs=(
            P(("groups", "gx"), "gy", "gz", None, None),
            P(("groups", "gx"), "gy", "gz", None),
            P(("groups", "gx"), "gy", "gz", None),
            P(("groups", "gx"), "gy", "gz"),
            P(),
            P(),
        ),
        out_specs=(P(("groups", "gx"), "gy", "gz", None, None), P("groups")),
        check_vma=False,
    )
```

```python
import functools

import jax
import jax.numpy as jnp
from jax import lax
from jax.experimental import pallas as pl
from jax.experimental.pallas import tpu as pltpu
from jax.sharding import PartitionSpec as P

CELL_EDGE = 1.1
SOFTEN = 0.09
ENERGY_UNIT = 0.1
EDGE_V = 1.0 / (1.0 + SOFTEN)
E0 = EDGE_V**0.5
E3 = EDGE_V**3
UNROLL = 8
GROUPS = (
    ((1, -1, -1, 3), (1, 0, -1, 3), (0, 0, 0, 2)),
    ((1, 1, -1, 3), (0, 1, -1, 3)),
)
SELF_ROW = 6


def shifted(block, axis, distance):
    n = lax.axis_size(axis)
    route = [((i - distance) % n, i) for i in range(n)]
    return lax.ppermute(block, axis, route)


def from_both(first, last, axis):
    if lax.axis_size(axis) == 2:
        both = shifted(jnp.stack([first, last]), axis, 1)
        return both[0], both[1]
    return shifted(first, axis, -1), shifted(last, axis, 1)


def ring_sum(value, axis):
    total = value
    for distance in range(1, lax.axis_size(axis)):
        total = total + shifted(value, axis, distance)
    return total


def returned(first, last, energy, axis):
    if lax.axis_size(axis) != 2:
        return (*from_both(first, last, axis), ring_sum(energy, axis))
    slots = energy.shape[-1]
    rows = jnp.stack([first, last]).reshape(-1, slots)
    got = shifted(jnp.concatenate([rows, energy]), axis, 1)
    both = got[:-1].reshape(2, *first.shape)
    return both[0], both[1], energy + got[-1:]


def pair_kernel(cx, cy, cz, nt, scal_ref, type_ref, count_ref, ext_ref, c6_ref, c12_ref,
                force_ref, energy_ref, tcell, table, fa, fb, columns, flat):
    ey = cy + 2
    ez = cz + 2
    slots = 128
    force_ref[...] = jnp.zeros_like(force_ref)
    fa[...] = jnp.zeros_like(fa)
    fb[...] = jnp.zeros_like(fb)
    table[...] = jnp.zeros_like(table)
    c6 = c6_ref[...]
    c12 = c12_ref[...]
    c6 = (0.5 * ENERGY_UNIT) * (c6 + c6.T)
    c12 = (0.5 * ENERGY_UNIT) * (c12 + c12.T)
    both = jnp.concatenate([c12, c6], axis=0)
    high = both.astype(jnp.bfloat16)
    low = (both - high.astype(jnp.float32)).astype(jnp.bfloat16)
    left = jnp.concatenate([high, low], axis=1)
    ids = lax.broadcasted_iota(jnp.int32, (nt, slots), 0).astype(jnp.float32)

    def table_of(xy, carry):
        for z in range(ez):
            row = ext_ref[4, xy, z : z + 1, :]
            hot = (ids == row).astype(jnp.float32).astype(jnp.bfloat16)
            tcell[xy, z] = jnp.dot(
                left, jnp.concatenate([hot, hot], axis=0), preferred_element_type=jnp.float32
            )
        return carry

    lax.fori_loop(1, (cx + 1) * ey, table_of, 0)

    rows = lax.broadcasted_iota(jnp.int32, (8, slots), 0)
    lanes = lax.broadcasted_iota(jnp.int32, (8, slots), 1)
    self_lane = jnp.where(rows == SELF_ROW, lanes, slots)
    wide_lanes = lax.broadcasted_iota(jnp.int32, (slots, slots), 1)
    columns[...] = jnp.zeros_like(columns)

    def cell(c, e_sum):
        x = c // (cy * cz)
        y = (c // cz) % cy
        z = c % cz
        b_rows = []
        for g, runs in enumerate(GROUPS):
            comps = [[], [], [], []]
            r = 0
            for ox, oy, oz, length in runs:
                xy = (x + ox) * ey + y + 1 + oy
                z0 = z + 1 + oz
                for k in range(4):
                    comps[k].append(ext_ref[k, xy, pl.ds(z0, length), :])
                for j in range(length):
                    t = tcell.at[xy, z0 + j]
                    table[g, pl.ds(r, nt, stride=8), :] = t[:nt, :]
                    table[2 + g, pl.ds(r, nt, stride=8), :] = t[nt:, :]
                    r += 1
            if r < 8:
                for k in range(4):
                    comps[k].append(jnp.zeros((8 - r, slots), jnp.float32))
            full = [jnp.concatenate(p, axis=0) for p in comps]
            for k in range(3):
                off = jnp.zeros((8, slots), jnp.float32)
                r = 0
                for ox, oy, oz, length in runs:
                    for j in range(length):
                        o = (ox, oy, oz + j)[k]
                        if o:
                            off = jnp.where(rows == r, jnp.float32(o * CELL_EDGE), off)
                        r += 1
                full[k] = full[k] + off
            b_rows.append(full)
        n_atoms = count_ref[c]

        def fold(step):
            at = pl.ds(pl.multiple_of(step * UNROLL, UNROLL), UNROLL)
            for k in range(3):
                total = fa[k, pl.ds(0, UNROLL, stride=8), :]
                for s in range(1, 8):
                    total = total + fa[k, pl.ds(s, UNROLL, stride=8), :]
                fb[k, at, :] = total

        def atoms(step, carry):
            fold(step)
            acc = [list(carry[0:3]), list(carry[3:6])]
            e_acc = carry[6]
            for uu in range(UNROLL):
                i = step * UNROLL + uu
                at = c * (4 * slots) + i
                xi = scal_ref[at]
                yi = scal_ref[at + slots]
                zi = scal_ref[at + 2 * slots]
                qi = scal_ref[at + 3 * slots]
                ti = pl.multiple_of(type_ref[c * slots + i] * 8, 8)
                mine = None
                for g in range(2):
                    bx, by, bz, bq = b_rows[g]
                    c12p = table[g, pl.ds(ti, 8), :]
                    c6p = table[2 + g, pl.ds(ti, 8), :]
                    dx = bx - xi
                    dy = by - yi
                    dz = bz - zi
                    t = dx * dx + dy * dy + (dz * dz + SOFTEN)
                    s = lax.rsqrt(t)
                    v = s * s
                    z3 = v * v * v
                    w = jnp.maximum((1.0 + SOFTEN) - t, 0.0)
                    if g == 0:
                        w = jnp.where(self_lane > i, w, 0.0)
                    qq = bq * qi
                    cz12 = c12p * z3
                    y1 = cz12 - c6p
                    u = qq * (s - E0) + (z3 - E3) * (y1 + c12p * E3)
                    h = qq * s + (z3 * 6.0) * (y1 + cz12)
                    uw = u * w
                    e_acc = e_acc + uw * w
                    gg = w * (v * h * w) + 4.0 * uw
                    f = [gg * dx, gg * dy, gg * dz]
                    acc[g] = [p + q for p, q in zip(acc[g], f)]
                    mine = f if mine is None else [p + q for p, q in zip(mine, f)]
                for k in range(3):
                    fa[k, pl.ds(uu * 8, 8), :] = mine[k]
            return (*acc[0], *acc[1], e_acc)

        zero = jnp.zeros((8, slots), jnp.float32)
        steps = (n_atoms + UNROLL - 1) // UNROLL
        out = lax.fori_loop(0, steps, atoms, (zero,) * 6 + (e_sum,))
        fold(steps)
        for g, runs in enumerate(GROUPS):
            r = 0
            for ox, oy, oz, length in runs:
                xy = (x + ox) * ey + y + 1 + oy
                for k in range(3):
                    force_ref[k, xy, pl.ds(z + 1 + oz, length), :] += out[3 * g + k][r : r + length]
                r += length
        mine_lane = wide_lanes == c % slots
        for k in range(3):
            summed = jnp.sum(fb[k, pl.ds(UNROLL, slots), :], axis=1, keepdims=True)
            columns[k, c // slots] = jnp.where(mine_lane, summed, columns[k, c // slots])
        return out[6]

    n_cells = cx * cy * cz
    e = lax.fori_loop(0, n_cells, cell, jnp.zeros((8, slots), jnp.float32))
    energy_ref[...] = e
    for k in range(3):
        for part in range(columns.shape[1]):
            flat[pl.ds(part * slots, slots), :] = columns[k, part].T
        for xy in range(cx * cy):
            at = (xy // cy) * ey + xy % cy + 1
            for z in range(cz):
                c = xy * cz + z
                occupied = lanes[:1] < count_ref[c]
                force_ref[k, at, z + 1 : z + 2, :] -= jnp.where(occupied, flat[c : c + 1, :], 0.0)


def on_device(coords, charges, atom_types, counts, c6_table, c12_table):
    cx, cy, cz, _, slots = coords.shape
    nt = c6_table.shape[0]
    occ = jnp.arange(slots, dtype=jnp.int32) < counts[..., None]
    charge = jnp.where(occ, charges, 0.0)
    kind = jnp.where(occ, atom_types, nt)
    local = jnp.concatenate(
        [jnp.moveaxis(coords, 3, 0), charge[None], kind.astype(jnp.float32)[None]], axis=0
    )
    scal = jnp.concatenate([coords, ENERGY_UNIT * charge[..., None, :]], axis=3).reshape(-1)
    up = shifted(local[:, :1], "gx", -1)
    ext = jnp.concatenate([local, up], axis=1)
    above, below = from_both(ext[:, :, :1], ext[:, :, -1:], "gy")
    ext = jnp.concatenate([below, ext, above], axis=2)
    above, below = from_both(ext[:, :, :, :1], ext[:, :, :, -1:], "gz")
    ext = jnp.concatenate([below, ext, above], axis=3)
    parts = (cx * cy * cz + slots - 1) // slots
    ex, ey, ez = cx + 1, cy + 2, cz + 2
    vm = pl.BlockSpec(memory_space=pltpu.VMEM)
    sm = pl.BlockSpec(memory_space=pltpu.SMEM)
    forces, energy = pl.pallas_call(
        functools.partial(pair_kernel, cx, cy, cz, nt),
        out_shape=(
            jax.ShapeDtypeStruct((3, ex * ey, ez, slots), jnp.float32),
            jax.ShapeDtypeStruct((8, slots), jnp.float32),
        ),
        in_specs=[sm, sm, sm, vm, vm, vm],
        out_specs=(vm, vm),
        scratch_shapes=[
            pltpu.VMEM((ex * ey, ez, 2 * nt, slots), jnp.float32),
            pltpu.VMEM((4, (nt + 1) * 8, slots), jnp.float32),
            pltpu.VMEM((3, UNROLL * 8, slots), jnp.float32),
            pltpu.VMEM((3, UNROLL + slots, slots), jnp.float32),
            pltpu.VMEM((3, parts, slots, slots), jnp.float32),
            pltpu.VMEM((parts * slots, slots), jnp.float32),
        ],
        compiler_params=pltpu.CompilerParams(vmem_limit_bytes=48 * 2**20),
    )(scal, kind.reshape(-1), counts.reshape(-1), ext.reshape(5, ex * ey, ez, slots), c6_table, c12_table)
    energy = jnp.sum(energy, axis=0, keepdims=True)
    forces = forces.reshape(3, ex, ey, ez, slots)
    low, high = from_both(forces[:, :, :, :1], forces[:, :, :, -1:], "gz")
    energy = ring_sum(energy, "gx")
    forces = forces[:, :, :, 1:-1].at[:, :, :, -1:].add(low).at[:, :, :, :1].add(high)
    low, high, energy = returned(forces[:, :, :1], forces[:, :, -1:], energy, "gy")
    forces = forces[:, :, 1:-1].at[:, :, -1:].add(low).at[:, :, :1].add(high)
    back = shifted(forces[:, cx:], "gx", 1)
    forces = forces[:, :cx].at[:, :1].add(back)
    energy = jnp.sum(ring_sum(energy, "gz"))
    return jnp.moveaxis(forces, 0, 3), energy.reshape(1)


def solution(mesh):
    return jax.shard_map(
        on_device,
        mesh=mesh,
        in_specs=(
            P(("groups", "gx"), "gy", "gz", None, None),
            P(("groups", "gx"), "gy", "gz", None),
            P(("groups", "gx"), "gy", "gz", None),
            P(("groups", "gx"), "gy", "gz"),
            P(),
            P(),
        ),
        out_specs=(P(("groups", "gx"), "gy", "gz", None, None), P("groups")),
        check_vma=False,
    )
```
